32 devices in a mesh: dp: 4 (over x, core), sx: 2 (over y), sy: 4 (over z).
Axes of the slice: x: 2, y: 2, z: 4, core: 2. Of those that a mesh axis runs over, the one named last changes fastest.
Arguments:
- activations: bfloat16 [4, 16, 16, 2048], P('dp', 'sx', 'sy'), may hold values from -6 to 6
- preact: bfloat16 [4, 16, 16, 4096], P('dp', 'sx', 'sy'), may hold values from -6 to 6
- pooled_grad: bfloat16 [4, 8, 8, 2048], P('dp', 'sx', 'sy'), may hold values from -12 to 12
- weights: bfloat16 [27, 64, 128], replicated, may hold values from -0.109375 to 0.109375
Outputs:
- input_grad: bfloat16 [4, 16, 16, 2048], P('dp', 'sx', 'sy')
- weight_grad: float32 [27, 64, 128], replicated
- bias_grad: float32 [128], replicated
The draws below stay inside these ranges and needn't reach their ends.
All inputs are finite; a program needn't handle non-finite values.
Results may differ from the reference program's by a relative error of at most 0.0021.
Values may be sent and summed in bfloat16 or wider, within the bound.
A program may use at most 64 MiB of HBM per device.

```python
import jax
import jax.numpy as jnp
from jax import lax

CI = 64
CO = 128
SAMPLES = 4
NX = 16
NY = 16
NZ = 32


def steps_of(rng, extent, split, smallest, largest):
    def one(dim, blocks):
        draws = jax.random.uniform(jax.random.fold_in(jax.random.fold_in(rng, 6), dim), (blocks,), jnp.float32, smallest / len(split), largest / len(split))
        return jnp.repeat(jnp.exp(draws), extent[dim] // blocks).reshape((-1,) + (1,) * (len(extent) - dim - 1))

    gain = one(*split[0])
    for cut in split[1:]:
        gain = gain * one(*cut)
    return gain


def gaussian(key, extent, scale, reach, cuts=(), kind=jnp.bfloat16):
    gain = steps_of(key, extent, cuts, -0.22, 0.18) if cuts else 1.0
    drawn = jax.random.normal(key, extent, jnp.float32) * scale * gain
    return jnp.minimum(jnp.maximum(drawn, -reach), reach).astype(kind)


def setup_inputs(seed: int = 0) -> dict:
    seeds = jax.random.split(jax.random.key(seed), 5)
    activations = gaussian(seeds[0], (SAMPLES, NX, NY, NZ * CI), 1.0, 6.0, ((0, 4), (1, 2), (2, 4)))
    preact = gaussian(seeds[1], (SAMPLES, NX, NY, NZ * CO), 1.0, 6.0, ((0, 4), (1, 2), (2, 4)))
    pooled_grad = gaussian(seeds[2], (SAMPLES, NX // 2, NY // 2, (NZ // 2) * CO), 2.0, 12.0, ((0, 4), (1, 2), (2, 4)))
    weights = gaussian(seeds[3], (27, CI, CO), (27 * CO) ** -0.5, 0.109375)
    return dict(activations=activations, preact=preact, pooled_grad=pooled_grad, weights=weights)


stencil_offsets = [(ox, oy, oz) for ox in (-1, 0, 1) for oy in (-1, 0, 1) for oz in (-1, 0, 1)]


def reference(activations, preact, pooled_grad, weights):
    def per_sample(carry, items):
        weight_acc, bias_acc = carry
        acts, before, upper = items
        acts = acts.reshape(NX, NY, NZ, CI)
        upper = upper.reshape(NX // 2, NY // 2, NZ // 2, CO)
        grad_act = jnp.repeat(jnp.repeat(jnp.repeat(upper, 2, 0), 2, 1), 2, 2).astype(jnp.float32) * 0.125
        slope = jnp.where(before.reshape(NX, NY, NZ, CO) > 0, 1.0, 0.3).astype(jnp.float32)
        gate_grad = (grad_act * slope).astype(jnp.bfloat16)
        padded = jnp.pad(gate_grad, ((1, 1), (1, 1), (1, 1), (0, 0)))
        acts_flat = acts.reshape(-1, CI)
        input_acc = jnp.zeros((NX * NY * NZ, CI), jnp.float32)
        terms = []
        for index, offset in enumerate(stencil_offsets):
            ox, oy, oz = offset
            moved = padded[1 - ox:1 - ox + NX, 1 - oy:1 - oy + NY, 1 - oz:1 - oz + NZ, :].reshape(-1, CO)
            input_acc = input_acc + jnp.dot(moved, weights[index].T, preferred_element_type=jnp.float32)
            terms.append(jnp.dot(acts_flat.T, moved, preferred_element_type=jnp.float32))
        weight_acc = weight_acc + jnp.stack(terms, axis=0)
        bias_acc = bias_acc + jnp.sum(gate_grad.reshape(-1, CO).astype(jnp.float32), axis=0)
        return (weight_acc, bias_acc), input_acc.astype(jnp.bfloat16).reshape(NX, NY, NZ * CI)

    start = (jnp.zeros((27, CI, CO), jnp.float32), jnp.zeros((CO,), jnp.float32))
    (weight_acc, bias_acc), input_grad = lax.scan(per_sample, start, (activations, preact, pooled_grad))
    return input_grad, weight_acc / SAMPLES, bias_acc / SAMPLES
```

```python
import functools

import jax
import jax.numpy as jnp
from jax import lax
from jax.experimental import pallas as pl
from jax.experimental.pallas import tpu as pltpu
from jax.sharding import PartitionSpec as P

MESH = pl.DeviceIdType.MESH
AXES = ("dp", "sx", "sy")
ROWS = 8


def stage_kinds(sizes):
    count = dict(zip(AXES, sizes))
    kinds = []
    if count["dp"] % 2 == 0:
        kinds.append(("core", 2))
        kinds.append(("chip", count["dp"] // 2))
    else:
        kinds.append(("dp", count["dp"]))
    kinds.append(("sx", count["sx"]))
    kinds.append(("sy", count["sy"]))
    return [kind for kind in kinds if kind[1] > 1]


def plan_parts(units, sizes):
    kinds = stage_kinds(sizes)
    devices = sizes[0] * sizes[1] * sizes[2]
    granules = -(-units // devices)
    names = [kind[0] for kind in kinds]
    if granules == 1 or "chip" not in names or "sx" not in names:
        return [(0, granules * devices, kinds)]
    first = -(-granules // 2)
    chip, side = names.index("chip"), names.index("sx")
    other = list(kinds)
    other[chip], other[side] = kinds[side], kinds[chip]
    return [
        (0, first * devices, kinds),
        (first * devices, (granules - first) * devices, other),
    ]


def chunks_of(part):
    sizes, length = [], part[1]
    for _, count in part[2]:
        length //= count
        sizes.append(length)
    return sizes


def place():
    return tuple(lax.axis_index(axis) for axis in AXES)


def member(kind, here):
    d, x, y = here
    return {"core": d % 2, "chip": d // 2, "dp": d, "sx": x, "sy": y}[kind]


def peer(kind, here, index):
    d, x, y = here
    if kind == "core":
        return (d - d % 2 + index, x, y)
    if kind == "chip":
        return (2 * index + d % 2, x, y)
    if kind == "dp":
        return (index, x, y)
    if kind == "sx":
        return (d, index, y)
    return (d, x, index)


def body(sizes, parts, samples, gate_ref, act_ref, weights_ref, grad_ref, total_ref, *scratch):
    count_parts = len(parts)
    gcat, acc, halo_x, halo_y, corner, input_acc = scratch[:6]
    landing = scratch[6 : 6 + count_parts]
    halo_send, halo_recv = scratch[6 + count_parts : 8 + count_parts]
    sems = scratch[8 + count_parts :]
    cells_x, cells_y, cells_z, chan_out = gate_ref.shape
    offsets, chan_in, _ = weights_ref.shape
    cells = cells_x * cells_y * cells_z
    units = chan_in // ROWS
    bias_unit = offsets * units
    here = place()
    d, x, y = here
    kinds = stage_kinds(sizes)

    barrier = pltpu.get_barrier_semaphore()
    greeted = 0
    for kind, count in kinds:
        for turn in range(1, count):
            target = peer(kind, here, (member(kind, here) + turn) % count)
            pl.semaphore_signal(barrier, inc=1, device_id=target, device_id_type=MESH)
            greeted += 1
    diagonals = [(dx, dy) for dx in (-1, 1) for dy in (-1, 1)]

    def inside(dx, dy):
        ok = None
        for coord, step, size in ((x, dx, sizes[1]), (y, dy, sizes[2])):
            if step == -1:
                term = coord > 0
            elif step == 1:
                term = coord < size - 1
            else:
                continue
            ok = term if ok is None else jnp.logical_and(ok, term)
        return ok

    for dx, dy in diagonals:
        @pl.when(inside(dx, dy))
        def _():
            pl.semaphore_signal(
                barrier, inc=1, device_id=(d, x + dx, y + dy), device_id_type=MESH
            )
    for dx, dy in diagonals:
        greeted = greeted + jnp.where(inside(dx, dy), 1, 0)
    pl.semaphore_wait(barrier, greeted)

    def side(step):
        return 0 if step == -1 else 1

    def edge(step, size):
        return 0 if step == -1 else size - 1

    def halo_copy(dx, dy):
        if dy == 0:
            src = gate_ref.at[edge(dx, cells_x)]
            dst = halo_x.at[side(-dx)]
            slot = side(dx)
            back = side(-dx)
        elif dx == 0:
            src = gate_ref.at[:, edge(dy, cells_y)]
            dst = halo_y.at[side(-dy)]
            slot = 2 + side(dy)
            back = 2 + side(-dy)
        else:
            src = gate_ref.at[edge(dx, cells_x), edge(dy, cells_y)]
            dst = corner.at[2 * side(-dx) + side(-dy)]
            slot = 4 + 2 * side(dx) + side(dy)
            back = 4 + 2 * side(-dx) + side(-dy)
        return pltpu.make_async_remote_copy(
            src_ref=src,
            dst_ref=dst,
            send_sem=halo_send.at[slot],
            recv_sem=halo_recv.at[back],
            device_id=(d, x + dx, y + dy),
            device_id_type=MESH,
        )

    ways = [(0, -1), (0, 1), (-1, 0), (1, 0)] + diagonals
    for dx, dy in ways:
        @pl.when(inside(dx, dy))
        def _():
            halo_copy(dx, dy).start()

    def widen(block):
        shape = block.shape
        wide = block.astype(jnp.float32).reshape(-1, cells_z, chan_out)
        depth = lax.broadcasted_iota(jnp.int32, wide.shape, 1)
        low = jnp.where(depth == cells_z - 1, 0.0, pltpu.roll(wide, cells_z - 1, 1))
        high = jnp.where(depth == 0, 0.0, pltpu.roll(wide, 1, 1))
        return jnp.concatenate(
            [low.astype(jnp.bfloat16), block.reshape(wide.shape), high.astype(jnp.bfloat16)],
            axis=-1,
        ).reshape(shape[:-1] + (3 * chan_out,))

    bias = jnp.zeros((ROWS, chan_out), jnp.float32)
    for row in range(cells_x):
        block = gate_ref[row]
        gcat[1 + row, pl.ds(1, cells_y)] = widen(block)
        bias = bias + jnp.sum(block.astype(jnp.float32).reshape(-1, ROWS, chan_out), axis=0)
    bias = jnp.sum(bias, axis=0, keepdims=True)
    top = lax.broadcasted_iota(jnp.int32, (ROWS, chan_out), 0) == 0
    acc[bias_unit] = jnp.where(top, jnp.broadcast_to(bias, (ROWS, chan_out)), 0.0)
    spare = acc.shape[0] - bias_unit - 1
    if spare:
        acc[pl.ds(bias_unit + 1, spare)] = jnp.zeros((spare, ROWS, chan_out), jnp.float32)

    for dx, dy in ways:
        ex = slice(1, 1 + cells_x) if dx == 0 else (0 if dx == -1 else cells_x + 1)
        ey = slice(1, 1 + cells_y) if dy == 0 else (0 if dy == -1 else cells_y + 1)

        @pl.when(inside(dx, dy))
        def _():
            halo_copy(-dx, -dy).wait_recv()
            if dy == 0:
                gcat[ex, ey] = widen(halo_x[side(dx)])
            elif dx == 0:
                gcat[ex, ey] = widen(halo_y[side(dy)])
            else:
                gcat[ex, ey] = widen(corner[2 * side(dx) + side(dy)])

        @pl.when(jnp.logical_not(inside(dx, dy)))
        def _():
            ref = gcat.at[ex, ey]
            ref[...] = jnp.zeros(ref.shape, jnp.bfloat16)

    started = []
    chunk_sizes = [chunks_of(part) for part in parts]
    starts = [[jnp.int32(part[0])] for part in parts]

    def slot_of(p, stage, turn):
        base = sum(count - 1 for _, count in parts[p][2][:stage])
        return base + turn - 1

    def row_of(p, stage, turn):
        base = 0
        for earlier in range(stage):
            base += (parts[p][2][earlier][1] - 1) * chunk_sizes[p][earlier]
        return base + (turn - 1) * chunk_sizes[p][stage]

    pending = [None] * count_parts

    def send_reduce(p, stage):
        kind, count = parts[p][2][stage]
        chunk = chunk_sizes[p][stage]
        me = member(kind, here)
        copies = []
        for turn in range(1, count):
            index = (me + turn) % count
            slot = slot_of(p, stage, turn)
            copy = pltpu.make_async_remote_copy(
                src_ref=acc.at[pl.ds(starts[p][-1] + index * chunk, chunk)],
                dst_ref=landing[p].at[pl.ds(row_of(p, stage, turn), chunk)],
                send_sem=sems[2 * p].at[0, slot],
                recv_sem=sems[2 * p + 1].at[0, slot],
                device_id=peer(kind, here, index),
                device_id_type=MESH,
            )
            copy.start()
            copies.append(copy)
            started.append(copy)
        pending[p] = copies

    def take_reduce(p, stage):
        kind, count = parts[p][2][stage]
        chunk = chunk_sizes[p][stage]
        own = starts[p][-1] + member(kind, here) * chunk
        starts[p].append(own)
        value = acc[pl.ds(own, chunk)]
        for turn in range(1, count):
            pending[p][turn - 1].wait_recv()
            value = value + landing[p][pl.ds(row_of(p, stage, turn), chunk)]
        acc[pl.ds(own, chunk)] = value

    def round_shard(p):
        own, chunk = starts[p][-1], chunk_sizes[p][-1]
        value = acc[pl.ds(own, chunk)] * (1.0 / (samples * sizes[0]))
        high = value.astype(jnp.bfloat16).astype(jnp.float32)
        rest = pltpu.roll(value - high, 1, 1)
        unit = own + lax.broadcasted_iota(jnp.int32, value.shape, 0)
        row = lax.broadcasted_iota(jnp.int32, value.shape, 1)
        kept = jnp.where(jnp.logical_and(unit == bias_unit, row == 1), rest, high)
        total_ref[pl.ds(own, chunk)] = kept.astype(jnp.bfloat16)

    def send_gather(p, stage):
        kind, count = parts[p][2][stage]
        chunk = chunk_sizes[p][stage]
        own = starts[p][stage + 1]
        me = member(kind, here)
        copies = []
        for turn in range(1, count):
            slot = slot_of(p, stage, turn)
            copy = pltpu.make_async_remote_copy(
                src_ref=total_ref.at[pl.ds(own, chunk)],
                dst_ref=total_ref.at[pl.ds(own, chunk)],
                send_sem=sems[2 * p].at[1, slot],
                recv_sem=sems[2 * p + 1].at[1, slot],
                device_id=peer(kind, here, (me + turn) % count),
                device_id_type=MESH,
            )
            copy.start()
            copies.append(copy)
            started.append(copy)
        pending[p] = copies

    ready = 0
    for a in (-1, 0, 1):
        for b in (-1, 0, 1):
            first = 9 * (a + 1) + 3 * (b + 1)
            moved = gcat[pl.ds(1 - a, cells_x), pl.ds(1 - b, cells_y)]
            term = jnp.dot(
                act_ref[...],
                moved.reshape(cells, 3 * chan_out),
                preferred_element_type=jnp.float32,
            )
            for c in range(3):
                acc[pl.ds((first + c) * units, units)] = term[
                    :, c * chan_out : (c + 1) * chan_out
                ].reshape(units, ROWS, chan_out)
            done = (first + 3) * units
            while ready < count_parts - 1 and parts[ready][0] + parts[ready][1] <= done:
                send_reduce(ready, 0)
                ready += 1
    while ready < count_parts:
        send_reduce(ready, 0)
        ready += 1

    def input_piece(a):
        total = None
        for b in (-1, 0, 1):
            first = 9 * (a + 1) + 3 * (b + 1)
            moved = gcat[pl.ds(1 - a, cells_x), pl.ds(1 - b, cells_y)]
            wide = jnp.concatenate([weights_ref[first + c] for c in range(3)], axis=1)
            term = lax.dot_general(
                moved.reshape(cells, 3 * chan_out),
                wide,
                (((1,), (1,)), ((), ())),
                preferred_element_type=jnp.float32,
            )
            total = term if total is None else total + term
        if a == -1:
            input_acc[...] = total
        elif a == 0:
            input_acc[...] += total
        else:
            grad_ref[...] = (input_acc[...] + total).astype(jnp.bfloat16)

    pieces = [-1, 0, 1]
    stages = len(kinds)
    for stage in range(stages):
        if pieces:
            input_piece(pieces.pop(0))
        for p in range(count_parts):
            take_reduce(p, stage)
            if stage + 1 < stages:
                send_reduce(p, stage + 1)
            else:
                round_shard(p)
                send_gather(p, stage)
    for a in pieces:
        input_piece(a)
    for stage in reversed(range(stages)):
        for p in range(count_parts):
            for copy in pending[p]:
                copy.wait_recv()
            if stage:
                send_gather(p, stage - 1)
    for copy in started:
        copy.wait_send()
    for dx, dy in ways:
        @pl.when(inside(dx, dy))
        def _():
            halo_copy(dx, dy).wait_send()


def fused(gate, acts, weights, samples, sizes):
    cells_x, cells_y, cells_z, chan_out = gate.shape
    offsets, chan_in, _ = weights.shape
    needed = offsets * chan_in // ROWS + 1
    parts = plan_parts(needed, sizes)
    units = sum(part[1] for part in parts)
    scratch = [
        pltpu.VMEM((cells_x + 2, cells_y + 2, cells_z, 3 * chan_out), jnp.bfloat16),
        pltpu.VMEM((units, ROWS, chan_out), jnp.float32),
        pltpu.VMEM((2, cells_y, cells_z, chan_out), jnp.bfloat16),
        pltpu.VMEM((2, cells_x, cells_z, chan_out), jnp.bfloat16),
        pltpu.VMEM((4, cells_z, chan_out), jnp.bfloat16),
        pltpu.VMEM((acts.shape[1], chan_in), jnp.float32),
    ]
    for part in parts:
        rows = sum(
            (count - 1) * chunk for (_, count), chunk in zip(part[2], chunks_of(part))
        )
        scratch.append(pltpu.VMEM((rows, ROWS, chan_out), jnp.float32))
    scratch += [pltpu.SemaphoreType.DMA((8,)), pltpu.SemaphoreType.DMA((8,))]
    for part in parts:
        slots = sum(count - 1 for _, count in part[2])
        scratch += [pltpu.SemaphoreType.DMA((2, slots)), pltpu.SemaphoreType.DMA((2, slots))]
    return pl.pallas_call(
        functools.partial(body, sizes, parts, samples),
        out_shape=(
            jax.ShapeDtypeStruct((acts.shape[1], chan_in), jnp.bfloat16),
            jax.ShapeDtypeStruct((units, ROWS, chan_out), jnp.bfloat16),
        ),
        in_specs=[pl.BlockSpec(memory_space=pltpu.VMEM)] * 3,
        out_specs=(pl.BlockSpec(memory_space=pltpu.VMEM),) * 2,
        scratch_shapes=scratch,
        compiler_params=pltpu.CompilerParams(
            collective_id=0, has_side_effects=True, vmem_limit_bytes=48 * 1024 * 1024
        ),
    )(gate, acts, weights)


def on_device(sizes, activations, preact, pooled_grad, weights):
    samples, cells_x, cells_y, flat_in = activations.shape
    offsets, chan_in, chan_out = weights.shape
    cells_z = flat_in // chan_in
    rows_x = samples * cells_x
    upper = pooled_grad.reshape(rows_x // 2, cells_y // 2, cells_z // 2, chan_out)
    grad_act = (
        jnp.repeat(jnp.repeat(jnp.repeat(upper, 2, 0), 2, 1), 2, 2).astype(jnp.float32) * 0.125
    )
    slope = jnp.where(
        preact.reshape(rows_x, cells_y, cells_z, chan_out) > 0, 1.0, 0.3
    ).astype(jnp.float32)
    gate = (grad_act * slope).astype(jnp.bfloat16)
    acts = activations.reshape(-1, chan_in).T
    grad, total = fused(gate, acts, weights, samples, sizes)
    input_grad = grad.reshape(activations.shape)
    unit = offsets * chan_in // ROWS
    weight_grad = total[:unit].astype(jnp.float32).reshape(offsets, chan_in, chan_out)
    bias = total[unit].astype(jnp.float32)
    return (input_grad, weight_grad, bias[0] + bias[1])


def solution(mesh):
    sizes = tuple(mesh.shape[axis] for axis in AXES)
    placed = (P("dp", "sx", "sy", None), P("dp", "sx", "sy", None), P("dp", "sx", "sy", None), P())
    return jax.shard_map(
        functools.partial(on_device, sizes),
        mesh=mesh,
        in_specs=placed,
        out_specs=(P("dp", "sx", "sy", None), P(), P()),
        check_vma=False,
    )
```

```python
import functools
import itertools

import jax
import jax.numpy as jnp
from jax import lax
from jax.experimental import pallas as pl
from jax.experimental.pallas import tpu as pltpu
from jax.sharding import PartitionSpec as P

MESH = pl.DeviceIdType.MESH
AXES = ("dp", "sx", "sy")
ROWS = 8


FACTORS = ("core", "chip", "sx", "sy")
GROUPS = (
    (("core", "chip", "sx"), ("sy",)),
    (("core", "sy"), ("chip", "sx")),
)
CODE = 2.0**36


def stage_kinds(sizes, groups):
    kinds = []
    for group in groups:
        count = 1
        for name in group:
            count *= span(name, sizes)
        if count > 1:
            kinds.append((group, count))
    return kinds


def span(name, sizes):
    pair = 2 if sizes[0] % 2 == 0 else 1
    return {"core": pair, "chip": sizes[0] // pair, "sx": sizes[1], "sy": sizes[2]}[name]


def plan_parts(units, sizes):
    devices = sizes[0] * sizes[1] * sizes[2]
    granules = -(-units // devices)
    count = min(len(GROUPS), granules)
    parts, first = [], 0
    for index in range(count):
        share = -(-(granules - first) // (count - index))
        parts.append((first * devices, share * devices, stage_kinds(sizes, GROUPS[index])))
        first += share
    return parts


def chunks_of(part):
    sizes, length = [], part[1]
    for _, count in part[2]:
        length //= count
        sizes.append(length)
    return sizes


def place():
    return tuple(lax.axis_index(axis) for axis in AXES)


def split(sizes, here):
    d, x, y = here
    pair = span("core", sizes)
    return {"core": d % pair, "chip": d // pair, "sx": x, "sy": y}


def member(sizes, group, here):
    values = split(sizes, here)
    index = 0
    for name in group:
        index = index * span(name, sizes) + values[name]
    return index


def peer(sizes, group, here, index):
    values = split(sizes, here)
    for name in reversed(group):
        values[name] = index % span(name, sizes)
        index = index // span(name, sizes)
    return (values["chip"] * span("core", sizes) + values["core"], values["sx"], values["sy"])


def meetings(sizes, parts):
    found = set()
    for part in parts:
        for group, _ in part[2]:
            ranges = [
                range(span(name, sizes)) if name in group else range(1) for name in FACTORS
            ]
            found.update(itertools.product(*ranges))
    found.discard((0,) * len(FACTORS))
    return sorted(found)


def moved_by(sizes, here, moves):
    values = split(sizes, here)
    for name, move in zip(FACTORS, moves):
        if move:
            values[name] = (values[name] + move) % span(name, sizes)
    return (values["chip"] * span("core", sizes) + values["core"], values["sx"], values["sy"])


def encode(value):
    scaled = value * CODE
    return (scaled * jnp.abs(scaled)).astype(jnp.bfloat16)


def decode(coded):
    wide = coded.astype(jnp.float32)
    root = jnp.sqrt(jnp.abs(wide)) * (1.0 / CODE)
    return jnp.where(wide < 0, -root, root)


def body(sizes, parts, samples, gate_ref, act_ref, weights_hbm, grad_ref, total_ref, *scratch):
    count_parts = len(parts)
    weights_ref = scratch[0]
    gcat, acc, halo_x, halo_y, corner, input_acc = scratch[1:7]
    landing = scratch[7 : 7 + count_parts]
    leaving = scratch[7 + count_parts : 7 + 2 * count_parts]
    halo_send, halo_recv, weight_sem = scratch[7 + 2 * count_parts : 10 + 2 * count_parts]
    sems = scratch[10 + 2 * count_parts :]
    weight_copy = pltpu.make_async_copy(weights_hbm, weights_ref, weight_sem)
    weight_copy.start()
    cells_x, cells_y, cells_z, chan_out = gate_ref.shape
    offsets, chan_in, _ = weights_hbm.shape
    cells = cells_x * cells_y * cells_z
    units = chan_in // ROWS
    bias_unit = offsets * units
    here = place()
    d, x, y = here

    barrier = pltpu.get_barrier_semaphore()
    greeted = 0
    for moves in meetings(sizes, parts):
        target = moved_by(sizes, here, moves)
        pl.semaphore_signal(barrier, inc=1, device_id=target, device_id_type=MESH)
        greeted += 1
    diagonals = [(dx, dy) for dx in (-1, 1) for dy in (-1, 1)]

    def inside(dx, dy):
        ok = None
        for coord, step, size in ((x, dx, sizes[1]), (y, dy, sizes[2])):
            if step == -1:
                term = coord > 0
            elif step == 1:
                term = coord < size - 1
            else:
                continue
            ok = term if ok is None else jnp.logical_and(ok, term)
        return ok

    for dx, dy in diagonals:
        @pl.when(inside(dx, dy))
        def _():
            pl.semaphore_signal(
                barrier, inc=1, device_id=(d, x + dx, y + dy), device_id_type=MESH
            )
    for dx, dy in diagonals:
        greeted = greeted + jnp.where(inside(dx, dy), 1, 0)
    pl.semaphore_wait(barrier, greeted)

    def side(step):
        return 0 if step == -1 else 1

    def edge(step, size):
        return 0 if step == -1 else size - 1

    def halo_copy(dx, dy):
        if dy == 0:
            src = gate_ref.at[edge(dx, cells_x)]
            dst = halo_x.at[side(-dx)]
            slot = side(dx)
            back = side(-dx)
        elif dx == 0:
            src = gate_ref.at[:, edge(dy, cells_y)]
            dst = halo_y.at[side(-dy)]
            slot = 2 + side(dy)
            back = 2 + side(-dy)
        else:
            src = gate_ref.at[edge(dx, cells_x), edge(dy, cells_y)]
            dst = corner.at[2 * side(-dx) + side(-dy)]
            slot = 4 + 2 * side(dx) + side(dy)
            back = 4 + 2 * side(-dx) + side(-dy)
        return pltpu.make_async_remote_copy(
            src_ref=src,
            dst_ref=dst,
            send_sem=halo_send.at[slot],
            recv_sem=halo_recv.at[back],
            device_id=(d, x + dx, y + dy),
            device_id_type=MESH,
        )

    ways = [(0, -1), (0, 1), (-1, 0), (1, 0)] + diagonals
    for dx, dy in ways:
        @pl.when(inside(dx, dy))
        def _():
            halo_copy(dx, dy).start()

    def widen(block):
        shape = block.shape
        wide = block.astype(jnp.float32).reshape(-1, cells_z, chan_out)
        depth = lax.broadcasted_iota(jnp.int32, wide.shape, 1)
        low = jnp.where(depth == cells_z - 1, 0.0, pltpu.roll(wide, cells_z - 1, 1))
        high = jnp.where(depth == 0, 0.0, pltpu.roll(wide, 1, 1))
        return jnp.concatenate(
            [low.astype(jnp.bfloat16), block.reshape(wide.shape), high.astype(jnp.bfloat16)],
            axis=-1,
        ).reshape(shape[:-1] + (3 * chan_out,))

    bias = jnp.zeros((ROWS, chan_out), jnp.float32)
    for row in range(cells_x):
        block = gate_ref[row]
        gcat[1 + row, pl.ds(1, cells_y)] = widen(block)
        bias = bias + jnp.sum(block.astype(jnp.float32).reshape(-1, ROWS, chan_out), axis=0)
    bias = jnp.sum(bias, axis=0, keepdims=True)
    top = lax.broadcasted_iota(jnp.int32, (ROWS, chan_out), 0) == 0
    acc[bias_unit] = jnp.where(top, jnp.broadcast_to(bias, (ROWS, chan_out)), 0.0)
    spare = acc.shape[0] - bias_unit - 1
    if spare:
        acc[pl.ds(bias_unit + 1, spare)] = jnp.zeros((spare, ROWS, chan_out), jnp.float32)

    for dx, dy in ways:
        ex = slice(1, 1 + cells_x) if dx == 0 else (0 if dx == -1 else cells_x + 1)
        ey = slice(1, 1 + cells_y) if dy == 0 else (0 if dy == -1 else cells_y + 1)

        @pl.when(inside(dx, dy))
        def _():
            halo_copy(-dx, -dy).wait_recv()
            if dy == 0:
                gcat[ex, ey] = widen(halo_x[side(dx)])
            elif dx == 0:
                gcat[ex, ey] = widen(halo_y[side(dy)])
            else:
                gcat[ex, ey] = widen(corner[2 * side(dx) + side(dy)])

        @pl.when(jnp.logical_not(inside(dx, dy)))
        def _():
            ref = gcat.at[ex, ey]
            ref[...] = jnp.zeros(ref.shape, jnp.bfloat16)

    started = []
    chunk_sizes = [chunks_of(part) for part in parts]
    starts = [[jnp.int32(part[0])] for part in parts]

    def slot_of(p, stage, turn):
        base = sum(count - 1 for _, count in parts[p][2][:stage])
        return base + turn - 1

    def row_of(p, stage, turn):
        base = 0
        for earlier in range(stage):
            base += (parts[p][2][earlier][1] - 1) * chunk_sizes[p][earlier]
        return base + (turn - 1) * chunk_sizes[p][stage]

    pending = [None] * count_parts

    def send_reduce(p, stage):
        kind, count = parts[p][2][stage]
        chunk = chunk_sizes[p][stage]
        me = member(sizes, kind, here)
        copies = []
        for turn in range(1, count):
            index = (me + turn) % count
            slot = slot_of(p, stage, turn)
            rows = pl.ds(row_of(p, stage, turn), chunk)
            leaving[p][rows] = encode(acc[pl.ds(starts[p][-1] + index * chunk, chunk)])
            copy = pltpu.make_async_remote_copy(
                src_ref=leaving[p].at[rows],
                dst_ref=landing[p].at[rows],
                send_sem=sems[2 * p].at[0, slot],
                recv_sem=sems[2 * p + 1].at[0, slot],
                device_id=peer(sizes, kind, here, index),
                device_id_type=MESH,
            )
            copy.start()
            copies.append(copy)
            started.append(copy)
        pending[p] = copies

    def take_reduce(p, stage):
        kind, count = parts[p][2][stage]
        chunk = chunk_sizes[p][stage]
        own = starts[p][-1] + member(sizes, kind, here) * chunk
        starts[p].append(own)
        value = acc[pl.ds(own, chunk)]
        for turn in range(1, count):
            pending[p][turn - 1].wait_recv()
            value = value + decode(landing[p][pl.ds(row_of(p, stage, turn), chunk)])
        acc[pl.ds(own, chunk)] = value

    def round_shard(p):
        own, chunk = starts[p][-1], chunk_sizes[p][-1]
        value = acc[pl.ds(own, chunk)] * (1.0 / (samples * sizes[0]))
        coded = encode(value)
        rest = pltpu.roll(value - decode(coded), 1, 1)
        unit = own + lax.broadcasted_iota(jnp.int32, value.shape, 0)
        row = lax.broadcasted_iota(jnp.int32, value.shape, 1)
        is_rest = jnp.logical_and(unit == bias_unit, row == 1)
        total_ref[pl.ds(own, chunk)] = encode(jnp.where(is_rest, rest, value))

    def send_gather(p, stage):
        kind, count = parts[p][2][stage]
        chunk = chunk_sizes[p][stage]
        own = starts[p][stage + 1]
        me = member(sizes, kind, here)
        copies = []
        for turn in range(1, count):
            slot = slot_of(p, stage, turn)
            copy = pltpu.make_async_remote_copy(
                src_ref=total_ref.at[pl.ds(own, chunk)],
                dst_ref=total_ref.at[pl.ds(own, chunk)],
                send_sem=sems[2 * p].at[1, slot],
                recv_sem=sems[2 * p + 1].at[1, slot],
                device_id=peer(sizes, kind, here, (me + turn) % count),
                device_id_type=MESH,
            )
            copy.start()
            copies.append(copy)
            started.append(copy)
        pending[p] = copies

    ready = 0
    for a in (-1, 0, 1):
        for b in (-1, 0, 1):
            first = 9 * (a + 1) + 3 * (b + 1)
            moved = gcat[pl.ds(1 - a, cells_x), pl.ds(1 - b, cells_y)]
            term = jnp.dot(
                act_ref[...],
                moved.reshape(cells, 3 * chan_out),
                preferred_element_type=jnp.float32,
            )
            for c in range(3):
                acc[pl.ds((first + c) * units, units)] = term[
                    :, c * chan_out : (c + 1) * chan_out
                ].reshape(units, ROWS, chan_out)
            done = (first + 3) * units
            while ready < count_parts - 1 and parts[ready][0] + parts[ready][1] <= done:
                send_reduce(ready, 0)
                ready += 1
    while ready < count_parts:
        send_reduce(ready, 0)
        ready += 1

    def input_piece(a):
        total = None
        for b in (-1, 0, 1):
            first = 9 * (a + 1) + 3 * (b + 1)
            moved = gcat[pl.ds(1 - a, cells_x), pl.ds(1 - b, cells_y)]
            wide = jnp.concatenate([weights_ref[first + c] for c in range(3)], axis=1)
            term = lax.dot_general(
                moved.reshape(cells, 3 * chan_out),
                wide,
                (((1,), (1,)), ((), ())),
                preferred_element_type=jnp.float32,
            )
            total = term if total is None else total + term
        if a == -1:
            input_acc[...] = total
        elif a == 0:
            input_acc[...] += total
        else:
            grad_ref[...] = (input_acc[...] + total).astype(jnp.bfloat16)

    weight_copy.wait()
    pieces = [-1, 0, 1]
    stages = max(len(part[2]) for part in parts)
    for stage in range(stages):
        if pieces:
            input_piece(pieces.pop(0))
        for p in range(count_parts):
            take_reduce(p, stage)
            if stage + 1 < stages:
                send_reduce(p, stage + 1)
            else:
                round_shard(p)
                send_gather(p, stage)
    for a in pieces:
        input_piece(a)
    for stage in reversed(range(stages)):
        for p in range(count_parts):
            for copy in pending[p]:
                copy.wait_recv()
            if stage:
                send_gather(p, stage - 1)
    for copy in started:
        copy.wait_send()
    for dx, dy in ways:
        @pl.when(inside(dx, dy))
        def _():
            halo_copy(dx, dy).wait_send()


def fused(gate, acts, weights, samples, sizes):
    cells_x, cells_y, cells_z, chan_out = gate.shape
    offsets, chan_in, _ = weights.shape
    needed = offsets * chan_in // ROWS + 1
    parts = plan_parts(needed, sizes)
    units = sum(part[1] for part in parts)
    scratch = [
        pltpu.VMEM(weights.shape, weights.dtype),
        pltpu.VMEM((cells_x + 2, cells_y + 2, cells_z, 3 * chan_out), jnp.bfloat16),
        pltpu.VMEM((units, ROWS, chan_out), jnp.float32),
        pltpu.VMEM((2, cells_y, cells_z, chan_out), jnp.bfloat16),
        pltpu.VMEM((2, cells_x, cells_z, chan_out), jnp.bfloat16),
        pltpu.VMEM((4, cells_z, chan_out), jnp.bfloat16),
        pltpu.VMEM((acts.shape[1], chan_in), jnp.float32),
    ]
    for part in parts + parts:
        rows = sum(
            (count - 1) * chunk for (_, count), chunk in zip(part[2], chunks_of(part))
        )
        scratch.append(pltpu.VMEM((rows, ROWS, chan_out), jnp.bfloat16))
    scratch += [pltpu.SemaphoreType.DMA((8,)), pltpu.SemaphoreType.DMA((8,)), pltpu.SemaphoreType.DMA]
    for part in parts:
        slots = sum(count - 1 for _, count in part[2])
        scratch += [pltpu.SemaphoreType.DMA((2, slots)), pltpu.SemaphoreType.DMA((2, slots))]
    return pl.pallas_call(
        functools.partial(body, sizes, parts, samples),
        out_shape=(
            jax.ShapeDtypeStruct((acts.shape[1], chan_in), jnp.bfloat16),
            jax.ShapeDtypeStruct((units, ROWS, chan_out), jnp.bfloat16),
        ),
        in_specs=[pl.BlockSpec(memory_space=pltpu.VMEM)] * 2
        + [pl.BlockSpec(memory_space=pltpu.MemorySpace.HBM)],
        out_specs=(pl.BlockSpec(memory_space=pltpu.VMEM),) * 2,
        scratch_shapes=scratch,
        compiler_params=pltpu.CompilerParams(
            collective_id=0, has_side_effects=True, vmem_limit_bytes=48 * 1024 * 1024
        ),
    )(gate, acts, weights)


def on_device(sizes, activations, preact, pooled_grad, weights):
    samples, cells_x, cells_y, flat_in = activations.shape
    offsets, chan_in, chan_out = weights.shape
    cells_z = flat_in // chan_in
    rows_x = samples * cells_x
    upper = pooled_grad.reshape(rows_x // 2, cells_y // 2, cells_z // 2, chan_out)
    grad_act = (
        jnp.repeat(jnp.repeat(jnp.repeat(upper, 2, 0), 2, 1), 2, 2).astype(jnp.float32) * 0.125
    )
    slope = jnp.where(
        preact.reshape(rows_x, cells_y, cells_z, chan_out) > 0, 1.0, 0.3
    ).astype(jnp.float32)
    gate = (grad_act * slope).astype(jnp.bfloat16)
    acts = activations.reshape(-1, chan_in).T
    grad, total = fused(gate, acts, weights, samples, sizes)
    input_grad = grad.reshape(activations.shape)
    unit = offsets * chan_in // ROWS
    weight_grad = decode(total[:unit]).reshape(offsets, chan_in, chan_out)
    bias = decode(total[unit])
    return (input_grad, weight_grad, bias[0] + bias[1])


def solution(mesh):
    sizes = tuple(mesh.shape[axis] for axis in AXES)
    placed = (P("dp", "sx", "sy", None), P("dp", "sx", "sy", None), P("dp", "sx", "sy", None), P())
    return jax.shard_map(
        functools.partial(on_device, sizes),
        mesh=mesh,
        in_specs=placed,
        out_specs=(P("dp", "sx", "sy", None), P(), P()),
        check_vma=False,
    )
```

```python
import functools
import itertools

import jax
import jax.numpy as jnp
from jax import lax
from jax.experimental import pallas as pl
from jax.experimental.pallas import tpu as pltpu
from jax.sharding import PartitionSpec as P

MESH = pl.DeviceIdType.MESH
AXES = ("dp", "sx", "sy")
ROWS = 8


FACTORS = ("core", "chip", "sx", "sy")
GROUPS = ((("core","chip","sx"), ("sy",)), (("core","sy"),("chip","sx")), (("core","chip","sx"), ("sy",)),)
CODE = 2.0**36


def stage_kinds(sizes, groups):
    kinds = []
    for group in groups:
        count = 1
        for name in group:
            count *= span(name, sizes)
        if count > 1:
            kinds.append((group, count))
    return kinds


def span(name, sizes):
    pair = 2 if sizes[0] % 2 == 0 else 1
    return {"core": pair, "chip": sizes[0] // pair, "sx": sizes[1], "sy": sizes[2]}[name]


def plan_parts(units, sizes):
    devices = sizes[0] * sizes[1] * sizes[2]
    granules = -(-units // devices)
    count = min(len(GROUPS), granules)
    parts, first = [], 0
    for index in range(count):
        share = -(-(granules - first) // (count - index))
        parts.append((first * devices, share * devices, stage_kinds(sizes, GROUPS[index])))
        first += share
    return parts


def chunks_of(part):
    sizes, length = [], part[1]
    for _, count in part[2]:
        length //= count
        sizes.append(length)
    return sizes


def place():
    return tuple(lax.axis_index(axis) for axis in AXES)


def split(sizes, here):
    d, x, y = here
    pair = span("core", sizes)
    return {"core": d % pair, "chip": d // pair, "sx": x, "sy": y}


def member(sizes, group, here):
    values = split(sizes, here)
    index = 0
    for name in group:
        index = index * span(name, sizes) + values[name]
    return index


def peer(sizes, group, here, index):
    values = split(sizes, here)
    for name in reversed(group):
        values[name] = index % span(name, sizes)
        index = index // span(name, sizes)
    return (values["chip"] * span("core", sizes) + values["core"], values["sx"], values["sy"])


def meetings(sizes, parts):
    found = set()
    for part in parts:
        for group, _ in part[2]:
            ranges = [
                range(span(name, sizes)) if name in group else range(1) for name in FACTORS
            ]
            found.update(itertools.product(*ranges))
    found.discard((0,) * len(FACTORS))
    return sorted(found)


def moved_by(sizes, here, moves):
    values = split(sizes, here)
    for name, move in zip(FACTORS, moves):
        if move:
            values[name] = (values[name] + move) % span(name, sizes)
    return (values["chip"] * span("core", sizes) + values["core"], values["sx"], values["sy"])


def encode(value):
    scaled = value * CODE
    return (scaled * jnp.abs(scaled)).astype(jnp.bfloat16)


def decode(coded):
    wide = coded.astype(jnp.float32)
    root = jnp.sqrt(jnp.abs(wide)) * (1.0 / CODE)
    return jnp.where(wide < 0, -root, root)


def body(sizes, parts, samples, gate_ref, act_ref, weights_hbm, grad_ref, total_ref, *scratch):
    count_parts = len(parts)
    weights_ref = scratch[0]
    gcat, acc, halo_x, halo_y, corner, input_acc = scratch[1:7]
    landing = scratch[7 : 7 + count_parts]
    leaving = scratch[7 + count_parts : 7 + 2 * count_parts]
    halo_send, halo_recv, weight_sem = scratch[7 + 2 * count_parts : 10 + 2 * count_parts]
    sems = scratch[10 + 2 * count_parts :]
    weight_copy = pltpu.make_async_copy(weights_hbm, weights_ref, weight_sem)
    weight_copy.start()
    cells_x, cells_y, cells_z, chan_out = gate_ref.shape
    offsets, chan_in, _ = weights_hbm.shape
    cells = cells_x * cells_y * cells_z
    units = chan_in // ROWS
    bias_unit = offsets * units
    here = place()
    d, x, y = here

    barrier = pltpu.get_barrier_semaphore()
    greeted = 0
    for moves in meetings(sizes, parts):
        target = moved_by(sizes, here, moves)
        pl.semaphore_signal(barrier, inc=1, device_id=target, device_id_type=MESH)
        greeted += 1
    diagonals = [(dx, dy) for dx in (-1, 1) for dy in (-1, 1)]

    def inside(dx, dy):
        ok = None
        for coord, step, size in ((x, dx, sizes[1]), (y, dy, sizes[2])):
            if step == -1:
                term = coord > 0
            elif step == 1:
                term = coord < size - 1
            else:
                continue
            ok = term if ok is None else jnp.logical_and(ok, term)
        return ok

    for dx, dy in diagonals:
        @pl.when(inside(dx, dy))
        def _():
            pl.semaphore_signal(
                barrier, inc=1, device_id=(d, x + dx, y + dy), device_id_type=MESH
            )
    for dx, dy in diagonals:
        greeted = greeted + jnp.where(inside(dx, dy), 1, 0)
    pl.semaphore_wait(barrier, greeted)

    def side(step):
        return 0 if step == -1 else 1

    def edge(step, size):
        return 0 if step == -1 else size - 1

    def halo_copy(dx, dy):
        if dy == 0:
            src = gate_ref.at[edge(dx, cells_x)]
            dst = halo_x.at[side(-dx)]
            slot = side(dx)
            back = side(-dx)
        elif dx == 0:
            src = gate_ref.at[:, edge(dy, cells_y)]
            dst = halo_y.at[side(-dy)]
            slot = 2 + side(dy)
            back = 2 + side(-dy)
        else:
            src = gate_ref.at[edge(dx, cells_x), edge(dy, cells_y)]
            dst = corner.at[2 * side(-dx) + side(-dy)]
            slot = 4 + 2 * side(dx) + side(dy)
            back = 4 + 2 * side(-dx) + side(-dy)
        return pltpu.make_async_remote_copy(
            src_ref=src,
            dst_ref=dst,
            send_sem=halo_send.at[slot],
            recv_sem=halo_recv.at[back],
            device_id=(d, x + dx, y + dy),
            device_id_type=MESH,
        )

    ways = [(0, -1), (0, 1), (-1, 0), (1, 0)] + diagonals
    for dx, dy in ways:
        @pl.when(inside(dx, dy))
        def _():
            halo_copy(dx, dy).start()

    def widen(block):
        shape = block.shape
        wide = block.astype(jnp.float32).reshape(-1, cells_z, chan_out)
        depth = lax.broadcasted_iota(jnp.int32, wide.shape, 1)
        low = jnp.where(depth == cells_z - 1, 0.0, pltpu.roll(wide, cells_z - 1, 1))
        high = jnp.where(depth == 0, 0.0, pltpu.roll(wide, 1, 1))
        return jnp.concatenate(
            [low.astype(jnp.bfloat16), block.reshape(wide.shape), high.astype(jnp.bfloat16)],
            axis=-1,
        ).reshape(shape[:-1] + (3 * chan_out,))

    bias = jnp.zeros((ROWS, chan_out), jnp.float32)
    for row in range(cells_x):
        block = gate_ref[row]
        gcat[1 + row, pl.ds(1, cells_y)] = widen(block)
        bias = bias + jnp.sum(block.astype(jnp.float32).reshape(-1, ROWS, chan_out), axis=0)
    bias = jnp.sum(bias, axis=0, keepdims=True)
    top = lax.broadcasted_iota(jnp.int32, (ROWS, chan_out), 0) == 0
    acc[bias_unit] = jnp.where(top, jnp.broadcast_to(bias, (ROWS, chan_out)), 0.0)
    spare = acc.shape[0] - bias_unit - 1
    if spare:
        acc[pl.ds(bias_unit + 1, spare)] = jnp.zeros((spare, ROWS, chan_out), jnp.float32)

    for dx, dy in ways:
        ex = slice(1, 1 + cells_x) if dx == 0 else (0 if dx == -1 else cells_x + 1)
        ey = slice(1, 1 + cells_y) if dy == 0 else (0 if dy == -1 else cells_y + 1)

        @pl.when(inside(dx, dy))
        def _():
            halo_copy(-dx, -dy).wait_recv()
            if dy == 0:
                gcat[ex, ey] = widen(halo_x[side(dx)])
            elif dx == 0:
                gcat[ex, ey] = widen(halo_y[side(dy)])
            else:
                gcat[ex, ey] = widen(corner[2 * side(dx) + side(dy)])

        @pl.when(jnp.logical_not(inside(dx, dy)))
        def _():
            ref = gcat.at[ex, ey]
            ref[...] = jnp.zeros(ref.shape, jnp.bfloat16)

    started = []
    chunk_sizes = [chunks_of(part) for part in parts]
    starts = [[jnp.int32(part[0])] for part in parts]

    def slot_of(p, stage, turn):
        base = sum(count - 1 for _, count in parts[p][2][:stage])
        return base + turn - 1

    def row_of(p, stage, turn):
        base = 0
        for earlier in range(stage):
            base += (parts[p][2][earlier][1] - 1) * chunk_sizes[p][earlier]
        return base + (turn - 1) * chunk_sizes[p][stage]

    pending = [None] * count_parts

    def send_reduce(p, stage):
        kind, count = parts[p][2][stage]
        chunk = chunk_sizes[p][stage]
        me = member(sizes, kind, here)
        copies = []
        for turn in range(1, count):
            index = (me + turn) % count
            slot = slot_of(p, stage, turn)
            rows = pl.ds(row_of(p, stage, turn), chunk)
            leaving[p][rows] = encode(acc[pl.ds(starts[p][-1] + index * chunk, chunk)])
            copy = pltpu.make_async_remote_copy(
                src_ref=leaving[p].at[rows],
                dst_ref=landing[p].at[rows],
                send_sem=sems[2 * p].at[0, slot],
                recv_sem=sems[2 * p + 1].at[0, slot],
                device_id=peer(sizes, kind, here, index),
                device_id_type=MESH,
            )
            copy.start()
            copies.append(copy)
            started.append(copy)
        pending[p] = copies

    def take_reduce(p, stage):
        kind, count = parts[p][2][stage]
        chunk = chunk_sizes[p][stage]
        own = starts[p][-1] + member(sizes, kind, here) * chunk
        starts[p].append(own)
        value = acc[pl.ds(own, chunk)]
        for turn in range(1, count):
            pending[p][turn - 1].wait_recv()
            value = value + decode(landing[p][pl.ds(row_of(p, stage, turn), chunk)])
        acc[pl.ds(own, chunk)] = value

    def round_shard(p):
        own, chunk = starts[p][-1], chunk_sizes[p][-1]
        value = acc[pl.ds(own, chunk)] * (1.0 / (samples * sizes[0]))
        coded = encode(value)
        rest = pltpu.roll(value - decode(coded), 1, 1)
        unit = own + lax.broadcasted_iota(jnp.int32, value.shape, 0)
        row = lax.broadcasted_iota(jnp.int32, value.shape, 1)
        is_rest = jnp.logical_and(unit == bias_unit, row == 1)
        total_ref[pl.ds(own, chunk)] = encode(jnp.where(is_rest, rest, value))

    def send_gather(p, stage):
        kind, count = parts[p][2][stage]
        chunk = chunk_sizes[p][stage]
        own = starts[p][stage + 1]
        me = member(sizes, kind, here)
        copies = []
        for turn in range(1, count):
            slot = slot_of(p, stage, turn)
            copy = pltpu.make_async_remote_copy(
                src_ref=total_ref.at[pl.ds(own, chunk)],
                dst_ref=total_ref.at[pl.ds(own, chunk)],
                send_sem=sems[2 * p].at[1, slot],
                recv_sem=sems[2 * p + 1].at[1, slot],
                device_id=peer(sizes, kind, here, (me + turn) % count),
                device_id_type=MESH,
            )
            copy.start()
            copies.append(copy)
            started.append(copy)
        pending[p] = copies

    ready = 0
    for a in (-1, 0, 1):
        for b in (-1, 0, 1):
            first = 9 * (a + 1) + 3 * (b + 1)
            moved = gcat[pl.ds(1 - a, cells_x), pl.ds(1 - b, cells_y)]
            term = jnp.dot(
                act_ref[...],
                moved.reshape(cells, 3 * chan_out),
                preferred_element_type=jnp.float32,
            )
            for c in range(3):
                acc[pl.ds((first + c) * units, units)] = term[
                    :, c * chan_out : (c + 1) * chan_out
                ].reshape(units, ROWS, chan_out)
            done = (first + 3) * units
            while ready < count_parts - 1 and parts[ready][0] + parts[ready][1] <= done:
                send_reduce(ready, 0)
                ready += 1
    while ready < count_parts:
        send_reduce(ready, 0)
        ready += 1

    def input_piece(a):
        total = None
        for b in (-1, 0, 1):
            first = 9 * (a + 1) + 3 * (b + 1)
            moved = gcat[pl.ds(1 - a, cells_x), pl.ds(1 - b, cells_y)]
            wide = jnp.concatenate([weights_ref[first + c] for c in range(3)], axis=1)
            term = lax.dot_general(
                moved.reshape(cells, 3 * chan_out),
                wide,
                (((1,), (1,)), ((), ())),
                preferred_element_type=jnp.float32,
            )
            total = term if total is None else total + term
        if a == -1:
            input_acc[...] = total
        elif a == 0:
            input_acc[...] += total
        else:
            grad_ref[...] = (input_acc[...] + total).astype(jnp.bfloat16)

    weight_copy.wait()
    pieces = [-1, 0, 1]
    stages = max(len(part[2]) for part in parts)
    for stage in range(stages):
        if pieces:
            input_piece(pieces.pop(0))
        for p in range(count_parts):
            take_reduce(p, stage)
            if stage + 1 < stages:
                send_reduce(p, stage + 1)
            else:
                round_shard(p)
                send_gather(p, stage)
    for a in pieces:
        input_piece(a)
    for stage in reversed(range(stages)):
        for p in range(count_parts):
            for copy in pending[p]:
                copy.wait_recv()
            if stage:
                send_gather(p, stage - 1)
    for copy in started:
        copy.wait_send()
    for dx, dy in ways:
        @pl.when(inside(dx, dy))
        def _():
            halo_copy(dx, dy).wait_send()


def fused(gate, acts, weights, samples, sizes):
    cells_x, cells_y, cells_z, chan_out = gate.shape
    offsets, chan_in, _ = weights.shape
    needed = offsets * chan_in // ROWS + 1
    parts = plan_parts(needed, sizes)
    units = sum(part[1] for part in parts)
    scratch = [
        pltpu.VMEM(weights.shape, weights.dtype),
        pltpu.VMEM((cells_x + 2, cells_y + 2, cells_z, 3 * chan_out), jnp.bfloat16),
        pltpu.VMEM((units, ROWS, chan_out), jnp.float32),
        pltpu.VMEM((2, cells_y, cells_z, chan_out), jnp.bfloat16),
        pltpu.VMEM((2, cells_x, cells_z, chan_out), jnp.bfloat16),
        pltpu.VMEM((4, cells_z, chan_out), jnp.bfloat16),
        pltpu.VMEM((acts.shape[1], chan_in), jnp.float32),
    ]
    for part in parts + parts:
        rows = sum(
            (count - 1) * chunk for (_, count), chunk in zip(part[2], chunks_of(part))
        )
        scratch.append(pltpu.VMEM((rows, ROWS, chan_out), jnp.bfloat16))
    scratch += [pltpu.SemaphoreType.DMA((8,)), pltpu.SemaphoreType.DMA((8,)), pltpu.SemaphoreType.DMA]
    for part in parts:
        slots = sum(count - 1 for _, count in part[2])
        scratch += [pltpu.SemaphoreType.DMA((2, slots)), pltpu.SemaphoreType.DMA((2, slots))]
    return pl.pallas_call(
        functools.partial(body, sizes, parts, samples),
        out_shape=(
            jax.ShapeDtypeStruct((acts.shape[1], chan_in), jnp.bfloat16),
            jax.ShapeDtypeStruct((units, ROWS, chan_out), jnp.bfloat16),
        ),
        in_specs=[pl.BlockSpec(memory_space=pltpu.VMEM)] * 2
        + [pl.BlockSpec(memory_space=pltpu.MemorySpace.HBM)],
        out_specs=(pl.BlockSpec(memory_space=pltpu.VMEM),) * 2,
        scratch_shapes=scratch,
        compiler_params=pltpu.CompilerParams(
            collective_id=0, has_side_effects=True, vmem_limit_bytes=48 * 1024 * 1024
        ),
    )(gate, acts, weights)


def on_device(sizes, activations, preact, pooled_grad, weights):
    samples, cells_x, cells_y, flat_in = activations.shape
    offsets, chan_in, chan_out = weights.shape
    cells_z = flat_in // chan_in
    rows_x = samples * cells_x
    upper = pooled_grad.reshape(rows_x // 2, cells_y // 2, cells_z // 2, chan_out)
    grad_act = (
        jnp.repeat(jnp.repeat(jnp.repeat(upper, 2, 0), 2, 1), 2, 2).astype(jnp.float32) * 0.125
    )
    slope = jnp.where(
        preact.reshape(rows_x, cells_y, cells_z, chan_out) > 0, 1.0, 0.3
    ).astype(jnp.float32)
    gate = (grad_act * slope).astype(jnp.bfloat16)
    acts = activations.reshape(-1, chan_in).T
    grad, total = fused(gate, acts, weights, samples, sizes)
    input_grad = grad.reshape(activations.shape)
    unit = offsets * chan_in // ROWS
    weight_grad = decode(total[:unit]).reshape(offsets, chan_in, chan_out)
    bias = decode(total[unit])
    return (input_grad, weight_grad, bias[0] + bias[1])


def solution(mesh):
    sizes = tuple(mesh.shape[axis] for axis in AXES)
    placed = (P("dp", "sx", "sy", None), P("dp", "sx", "sy", None), P("dp", "sx", "sy", None), P())
    return jax.shard_map(
        functools.partial(on_device, sizes),
        mesh=mesh,
        in_specs=placed,
        out_specs=(P("dp", "sx", "sy", None), P(), P()),
        check_vma=False,
    )
```
